32 devices in a mesh: grp: 2 (over x), view: 16 (over z, y, core).
Axes of the slice: x: 2, y: 2, z: 4, core: 2. Of those that a mesh axis runs over, the one named last changes fastest.
Arguments:
- features: float32 [32, 32, 8, 256], P(('grp', 'view')), parts along dimension 0, may hold values from -96 to 96, as said below
- offsets: int32 [32, 128], P(('grp', 'view')), parts along dimension 0, may hold values from 0 to 31
- conf_bins: int32 [16, 256], P('grp'), parts along dimension 0, may hold values from 0 to 3
- plane_depths: float32 [128], P('view'), may hold values from 1 to 10
Outputs:
- cost_volume: float32 [128, 16, 256], P('view', 'grp'), parts along dimension 1
- depth_map: float32 [16, 256], P('grp'), parts along dimension 0
The draws below stay inside these ranges and needn't reach their ends.
There are 2 independent parts, one for each index of `grp`. The reference program is written for one: setup_inputs(seed, part) draws one part's arguments, and reference() takes and returns one part's arrays. A program takes and returns all parts, laid end to end along the dimension named above; an argument that names none is the same for every part. Nothing has to cross between parts.
Inputs may be any that keep to these rules, and one draw needn't show every extreme that they name: `features`: feature entries may be large on some rows.
All inputs are finite; a program needn't handle non-finite values.
Results may differ from the reference program's by a relative error of at most 0.0003.
Values sent between devices are 32-bit elements; how exact they have to be, the bound alone decides.
A program may use at most 128 MiB of HBM per device.

```python
import jax
import jax.numpy as jnp
from jax import lax

C = 32
W = 256
PLANES = 128
ROWS = 8
ITERS = 4
VIEWS = 16


def draw_features(key, part):
    first = jax.random.fold_in(key, 0)
    third = jax.random.fold_in(key, 7)
    fourth = jax.random.fold_in(key, 11)
    fifth = jax.random.fold_in(key, 13)
    sixth = jax.random.fold_in(key, 17)
    noise = jnp.clip(jax.random.normal(first, (VIEWS, C, ROWS, W), jnp.float32), -6.0, 6.0)
    level = jnp.clip(jax.random.normal(fifth, (C, ROWS, 1), jnp.float32), -4.0, 4.0)
    shared = jnp.clip(jax.random.normal(sixth, (C, ROWS, W), jnp.float32), -6.0, 6.0)
    values = 0.7 * (level + shared)[None] + 0.7 * noise
    chosen_row = jax.random.randint(third, (), 0, ROWS)
    strength = jax.random.uniform(fourth, (), jnp.float32, 14.0, 24.0)
    row_marks = (jnp.arange(ROWS, dtype=jnp.int32) == chosen_row).astype(jnp.float32)
    row_scale = 1.0 + (strength - 1.0) * row_marks
    values = values * row_scale[:, None]
    return jnp.clip(values, -96.0, 96.0)


def set_ends(drawn, own_key, least, high):
    longest = drawn.shape.index(max(drawn.shape))
    spots = []
    for shift in (0, 1):
        where = [jax.random.randint(jax.random.fold_in(own_key, axis), (), 0, length) for axis, length in enumerate(drawn.shape)]
        where[longest] = (where[longest] + shift) % drawn.shape[longest]
        spots.append(tuple(where))
    return drawn.at[spots[0]].set(least).at[spots[1]].set(high)


def level_of(rng, shape, pieces, least, top_value):
    factor_of = 1.0
    for axis_at, shards_of in pieces:
        draws = jax.random.uniform(jax.random.fold_in(jax.random.fold_in(rng, 6), axis_at), (shards_of,), jnp.float32, least / len(pieces), top_value / len(pieces))
        factor_of = factor_of * jnp.repeat(jnp.exp(draws), shape[axis_at] // shards_of).reshape((-1,) + (1,) * (len(shape) - 1 - axis_at))
    return factor_of


def setup_inputs(seed: int = 0, part: int = 0) -> dict:
    key_list = jax.random.split(jax.random.key(seed), 5)
    part_splits = jax.random.split(jax.random.fold_in(key_list[4], part), 5)
    return {
        "features": draw_features(jax.random.fold_in(jax.random.fold_in(key_list[4], part), 71), part),
        "offsets": set_ends(jax.random.randint(part_splits[1], (VIEWS, PLANES), 0, W // 8), jax.random.fold_in(part_splits[1], 1), 0, (W // 8) - 1).astype(jnp.int32),
        "conf_bins": set_ends(jax.random.randint(part_splits[2], (ROWS, W), 0, 4), jax.random.fold_in(part_splits[2], 1), 0, 3).astype(jnp.int32),
        "plane_depths": jnp.clip(1.0 + 9.0 * jax.random.uniform(key_list[3], (PLANES,), jnp.float32) ** level_of(key_list[3], (PLANES,), ((0, 16),), -0.2, 0.2), 1.0, 10.0),
    }


def warp_tile(tile, shift):
    pad = tile.shape[2] // 8
    padded = jnp.pad(tile, ((0, 0), (0, 0), (pad, 0)))
    return lax.dynamic_slice_in_dim(padded, (pad - shift).astype(jnp.int32), tile.shape[2], 2)


def reference(features, offsets, conf_bins, plane_depths):
    count = features.shape[0]

    def one_plane(shifts):
        warped = jax.vmap(warp_tile)(features, shifts)
        total = jnp.sum(warped, axis=0)
        square = jnp.sum(warped * warped, axis=0)
        mean = total / count
        return jnp.mean(square / count - mean * mean, axis=0)

    cost = lax.map(one_plane, jnp.transpose(offsets))
    conf = (conf_bins.astype(jnp.float32) + 1.0) * 0.25
    for step in range(ITERS):
        padded = jnp.pad(cost, 1)
        beside = padded[2:, 1:-1, 1:-1] + padded[:-2, 1:-1, 1:-1]
        beside = beside + padded[1:-1, 2:, 1:-1] + padded[1:-1, :-2, 1:-1]
        beside = beside + padded[1:-1, 1:-1, 2:] + padded[1:-1, 1:-1, :-2]
        cost = cost + 0.15 * conf * (beside - 6.0 * cost)
    logits = -cost
    peak = jnp.max(logits, axis=0)
    weights = jnp.exp(logits - peak)
    depth = jnp.sum(weights * plane_depths[:, None, None], axis=0) / jnp.sum(weights, axis=0)
    return cost, depth
```

```python
import functools

import jax
import jax.numpy as jnp
from jax import lax
from jax.experimental import pallas as pl
from jax.experimental.pallas import tpu as pltpu
from jax.sharding import PartitionSpec as P

ITERS = 4
LANES = 128
GROUP = 8


def each(start, end, body):
    if end - start < 16:
        for k in range(start, end):
            body(k)
        return

    def step(k, carry):
        body(k)
        return carry

    lax.fori_loop(start, end, step, 0)


def portions(n):
    ends = [n * part // 16 for part in (5, 10, 14, 16)]
    starts = [0] + ends[:-1]
    return [(a, b) for a, b in zip(starts, ends) if b > a]


def kernel(
    n, feat_ref, off_ref, conf_ref, depth_ref, out_ref,
    feat, xs, xr, aux, deps, offv, offs, table, acc, sqs, picks, hots, part, costq, costs, rateq, rates, depcol, vs,
    local_sem, xs_send, xs_recv, aux_send, aux_recv, d_send, d_recv, c_send, c_recv, v_send, v_recv,
):
    _, chans, rows, width = feat_ref.shape
    planes = off_ref.shape[-1]
    owned = depth_ref.shape[0]
    groups = n // rows
    cg = chans // groups
    pad = width // 8
    halo = ITERS
    pix = width // n
    step = max(GROUP, pix)
    span = step + 2 * halo
    per_window = step // pix
    lanes_out = vs.shape[-1]
    chunks = width // LANES
    entry_rows = chunks * cg
    me = lax.axis_index("view")

    lane = lax.broadcasted_iota(jnp.int32, (cg, LANES), 1)

    def build(place, x):
        pieces = [x[:, c * LANES:(c + 1) * LANES] for c in range(chunks)]
        for o in range(pad):
            turned = [pltpu.roll(piece, o, 1) if o else piece for piece in pieces]
            for c in range(chunks):
                before = turned[c - 1] if c else jnp.zeros_like(turned[c])
                line = jnp.where(lane >= o, turned[c], before) if o else turned[c]
                table[place * pad + o, c * cg:(c + 1) * cg, :] = line
        sqs[pl.ds(place, 1), :] = jnp.sum(x * x, axis=0, keepdims=True)

    barrier = pltpu.get_barrier_semaphore()

    def greet(k, carry):
        pl.semaphore_signal(barrier, inc=1, device_id={"view": lax.rem(me + k, n)})
        return carry

    lax.fori_loop(1, n, greet, 0)
    fetch = pltpu.make_async_copy(feat_ref.at[0], feat, local_sem)
    fetch.start()
    plane_lane = lax.broadcasted_iota(jnp.int32, (1, planes), 1)
    depth_row = jnp.zeros((1, planes), jnp.float32)
    for i in range(owned):
        depth_row = jnp.where(plane_lane == me * owned + i, depth_ref[i], depth_row)
    aux[me] = off_ref[...]
    deps[me] = depth_row
    fetch.wait()
    for r in range(rows):
        line = feat[:, r, :]
        for g in range(groups):
            xs[r * groups + g] = line[g * cg:(g + 1) * cg]
    pl.semaphore_wait(barrier, n - 1)

    def aux_copy(slot, peer):
        return pltpu.make_async_remote_copy(
            src_ref=aux.at[slot], dst_ref=aux.at[slot], send_sem=aux_send.at[peer],
            recv_sem=aux_recv.at[slot], device_id={"view": peer})

    def dep_copy(slot, peer):
        return pltpu.make_async_remote_copy(
            src_ref=deps.at[slot], dst_ref=deps.at[slot], send_sem=d_send.at[peer],
            recv_sem=d_recv.at[slot], device_id={"view": peer})

    def feat_copy(slot, peer):
        return pltpu.make_async_remote_copy(
            src_ref=xs.at[peer], dst_ref=xr.at[slot], send_sem=xs_send.at[peer],
            recv_sem=xs_recv.at[slot], device_id={"view": peer})

    each(1, n, lambda k: aux_copy(me, lax.rem(me + k, n)).start())
    each(1, n, lambda k: feat_copy(me, lax.rem(me + k, n)).start())
    each(1, n, lambda k: dep_copy(me, lax.rem(me + k, n)).start())
    build(0, xs[me])

    conf = (conf_ref[...].astype(jnp.float32) + 1.0) * 0.25
    rate = 0.15 * conf
    rate = jnp.concatenate([rate, jnp.zeros((LANES - rows, width), jnp.float32)], axis=0)
    rateq[...] = jnp.zeros_like(rateq)
    rateq[halo:halo + width, :] = rate.T
    first_pixel = pl.multiple_of(me // per_window * step, GROUP)
    near = rateq[pl.ds(first_pixel, span), :]
    for r in range(rows):
        rates[r] = jnp.broadcast_to(near[:, r:r + 1], (span, planes))
    costq[0:GROUP, :] = jnp.zeros((GROUP, planes), jnp.float32)
    costq[width:width + 2 * halo, :] = jnp.zeros((2 * halo, planes), jnp.float32)
    part[...] = jnp.zeros_like(part)

    shift = lax.broadcasted_iota(jnp.int32, (pad, width), 0)
    inside = lax.broadcasted_iota(jnp.int32, (pad, width), 1) >= shift

    per_hot = LANES // pad

    def squares(h, start, end):
        lines = []
        for k in range(h * per_hot, (h + 1) * per_hot):
            if start <= k < end:
                line = jnp.broadcast_to(sqs[k:k + 1, :], (pad, width))
                line = pltpu.roll(line, 0, 1, stride=1, stride_axis=0)
                lines.append(jnp.where(inside, line, 0.0))
            else:
                lines.append(jnp.zeros((pad, width), jnp.float32))
        sq_all = jnp.concatenate(lines, axis=0)
        high = sq_all.astype(jnp.bfloat16)
        rest = sq_all - high.astype(jnp.float32)
        mid = rest.astype(jnp.bfloat16)
        low = (rest - mid.astype(jnp.float32)).astype(jnp.bfloat16)
        square = jnp.zeros((planes, width), jnp.float32)
        for piece in (low, mid, high):
            square = square + jnp.dot(hots[h], piece, preferred_element_type=jnp.float32)
        part[...] += square * (1.0 / (n * chans))

    def accumulate(start, end, is_last):
        def body(j, carry):
            sums = []
            for i in range(GROUP):
                p = j * GROUP + i
                total = acc[p] if start else None
                for k in range(start, end):
                    entry = table[offs[k, p]]
                    total = entry if total is None else total + entry
                if is_last:
                    total = total * total
                    sums.append(jnp.concatenate(
                        [jnp.sum(total[c * cg:(c + 1) * cg], axis=0, keepdims=True) for c in range(chunks)],
                        axis=1))
                else:
                    acc[p] = total
            if is_last:
                first = pl.multiple_of(j * GROUP, GROUP)
                part[pl.ds(first, GROUP), :] = (
                    part[pl.ds(first, GROUP), :]
                    - jnp.concatenate(sums, axis=0) * (1.0 / (n * n * chans)))
            return carry

        lax.fori_loop(0, planes // GROUP, body, 0)

    def take_offsets():
        each(1, n, lambda k: aux_copy(lax.rem(me - k + n, n), lax.rem(me - k + n, n)).wait_recv())
        for k in range(n):
            picks[k:k + 1, :] = aux[lax.rem(me - k + n, n)]
        places = lax.broadcasted_iota(jnp.int32, (n, planes), 0)
        offv[...] = picks[...] + places * pad
        to_scalar = pltpu.make_async_copy(offv, offs, local_sem)
        to_scalar.start()
        amount = lax.broadcasted_iota(jnp.int32, (pad, planes), 0)
        for h in range(n // per_hot):
            hot = jnp.concatenate(
                [jnp.where(picks[k:k + 1, :] == amount, 1.0, 0.0)
                 for k in range(h * per_hot, (h + 1) * per_hot)], axis=0)
            hots[h] = hot.T.astype(jnp.bfloat16)
        to_scalar.wait()

    for start, end in portions(n):
        first = max(start, 1)

        def receive(k, count):
            sources = [lax.rem(me - k - i + n, n) for i in range(count)]
            for source in sources:
                feat_copy(source, source).wait_recv()
            for i, source in enumerate(sources):
                build(k + i, xr[source])

        def receive_two(i, carry):
            receive(first + 2 * i, 2)
            return carry

        lax.fori_loop(0, (end - first) // 2, receive_two, 0)
        if (end - first) % 2:
            receive(end - 1, 1)
        if start == 0:
            take_offsets()
        for h in range(start // per_hot, (end - 1) // per_hot + 1):
            squares(h, start, end)
        accumulate(start, end, end == n)

    costq[halo:halo + width, :] = part[...].T

    def cost_copy(slot, peer):
        first = pl.multiple_of(peer // per_window * step, GROUP)
        return pltpu.make_async_remote_copy(
            src_ref=costq.at[pl.ds(first, span)], dst_ref=costs.at[slot],
            send_sem=c_send.at[peer], recv_sem=c_recv.at[slot], device_id={"view": peer})

    each(1, n, lambda k: cost_copy(me, lax.rem(me + k, n)).start())
    each(1, n, lambda k: dep_copy(lax.rem(me - k + n, n), lax.rem(me - k + n, n)).wait_recv())
    all_depths = jnp.sum(deps[:, 0, :], axis=0, keepdims=True)
    depcol[...] = jnp.broadcast_to(all_depths, (lanes_out, planes)).T
    costs[me] = costq[pl.ds(first_pixel, span), :]

    each(1, n, lambda k: cost_copy(lax.rem(me - k + n, n), lax.rem(me - k + n, n)).wait_recv())

    plane = lax.broadcasted_iota(jnp.int32, (span, planes), 1)
    cost = []
    for r in range(rows):
        total = costs[r * groups]
        for g in range(1, groups):
            total = total + costs[r * groups + g]
        cost.append(total)
    for _ in range(ITERS):
        new = []
        for r in range(rows):
            c = cost[r]
            beside = pltpu.roll(c, 1, 0) + pltpu.roll(c, span - 1, 0)
            if r > 0:
                beside = beside + cost[r - 1]
            if r < rows - 1:
                beside = beside + cost[r + 1]
            beside = beside + jnp.where(plane > 0, pltpu.roll(c, 1, 1), 0.0)
            beside = beside + jnp.where(plane < planes - 1, pltpu.roll(c, planes - 1, 1), 0.0)
            new.append(c + rates[r] * (beside - 6.0 * c))
        cost = new

    mine = []
    for r in range(rows):
        own = cost[r][halo:halo + pix]
        for m in range(1, per_window):
            first = halo + m * pix
            own = jnp.where(lax.rem(me, per_window) == m, cost[r][first:first + pix], own)
        mine.append(own)
    if lanes_out > rows * pix:
        mine.append(jnp.zeros((lanes_out - rows * pix, planes), jnp.float32))
    final = jnp.concatenate(mine, axis=0).T
    peak = jnp.max(-final, axis=0, keepdims=True)
    weight = jnp.exp(-final - peak)
    denom = jnp.sum(weight, axis=0, keepdims=True)
    numer = jnp.sum(weight * depcol[...], axis=0, keepdims=True)
    depth = numer / denom
    for j in range(n):
        vs[j, 0:owned, :] = final[j * owned:(j + 1) * owned]
        vs[j, owned:owned + 1, :] = depth

    def out_copy(slot, peer):
        return pltpu.make_async_remote_copy(
            src_ref=vs.at[peer], dst_ref=out_ref.at[slot],
            send_sem=v_send.at[peer], recv_sem=v_recv.at[slot], device_id={"view": peer})

    each(1, n, lambda k: out_copy(me, lax.rem(me + k, n)).start())
    out_ref[me] = vs[me]

    def finish(k, carry):
        peer = lax.rem(me + k, n)
        aux_copy(me, peer).wait_send()
        dep_copy(me, peer).wait_send()
        feat_copy(me, peer).wait_send()
        cost_copy(me, peer).wait_send()
        return carry

    lax.fori_loop(1, n, finish, 0)

    each(1, n, lambda k: out_copy(lax.rem(me - k + n, n), lax.rem(me - k + n, n)).wait_recv())
    each(1, n, lambda k: out_copy(me, lax.rem(me + k, n)).wait_send())


def lay_out(pieces, cost_out, map_out):
    n = pieces.shape[0]
    owned, rows, width = cost_out.shape
    pix = width // n
    per_chunk = LANES // pix
    lane = lax.broadcasted_iota(jnp.int32, (owned + 1, LANES), 1) // pix
    for c in range(width // LANES):
        for r in range(rows):
            line = None
            for k in range(per_chunk):
                piece = pieces[c * per_chunk + k]
                shift = (k - r) * pix % LANES
                if shift:
                    piece = pltpu.roll(piece, shift, 1)
                line = piece if line is None else jnp.where(lane == k, piece, line)
            cost_out[:, r, c * LANES:(c + 1) * LANES] = line[:owned]
            map_out[r:r + 1, c * LANES:(c + 1) * LANES] = line[owned:]


def per_device(features, offsets, conf_bins, plane_depths):
    n = lax.axis_size("view")
    _, chans, rows, width = features.shape
    planes = offsets.shape[-1]
    owned = plane_depths.shape[0]
    cg = chans * rows // n
    pad = width // 8
    pix = width // n
    span = max(GROUP, pix) + 2 * ITERS
    lanes_out = max(LANES, rows * pix)
    f32 = jnp.float32
    vmem = pl.BlockSpec(memory_space=pltpu.VMEM)
    dma = pltpu.SemaphoreType.DMA
    pieces = pl.pallas_call(
        functools.partial(kernel, n),
        out_shape=jax.ShapeDtypeStruct((n, owned + 1, lanes_out), f32),
        in_specs=[pl.BlockSpec(memory_space=pl.ANY), vmem, vmem, pl.BlockSpec(memory_space=pltpu.SMEM)],
        out_specs=vmem,
        scratch_shapes=[
            pltpu.VMEM((chans, rows, width), f32),
            pltpu.VMEM((n, cg, width), f32),
            pltpu.VMEM((n, cg, width), f32),
            pltpu.VMEM((n, 1, planes), jnp.int32),
            pltpu.VMEM((n, 1, planes), f32),
            pltpu.VMEM((n, planes), jnp.int32),
            pltpu.SMEM((n, planes), jnp.int32),
            pltpu.VMEM((n * pad, cg * width // LANES, LANES), f32),
            pltpu.VMEM((planes, cg * width // LANES, LANES), f32),
            pltpu.VMEM((n, width), f32),
            pltpu.VMEM((n, planes), jnp.int32),
            pltpu.VMEM((n * pad // LANES, planes, LANES), jnp.bfloat16),
            pltpu.VMEM((planes, width), f32),
            pltpu.VMEM((width + 2 * ITERS, planes), f32),
            pltpu.VMEM((n, span, planes), f32),
            pltpu.VMEM((width + 2 * ITERS, LANES), f32),
            pltpu.VMEM((rows, span, planes), f32),
            pltpu.VMEM((planes, lanes_out), f32),
            pltpu.VMEM((n, owned + 1, lanes_out), f32),
            dma,
        ] + [dma((n,)) for _ in range(10)],
        compiler_params=pltpu.CompilerParams(collective_id=0, has_side_effects=True,
                                             vmem_limit_bytes=60 << 20),
    )(features, offsets, conf_bins, plane_depths)
    return pl.pallas_call(
        lay_out,
        out_shape=(
            jax.ShapeDtypeStruct((owned, rows, width), f32),
            jax.ShapeDtypeStruct((rows, width), f32),
        ),
        in_specs=[vmem],
        out_specs=(vmem, vmem),
    )(pieces)


def solution(mesh):
    in_specs = (
        P(("grp", "view"), None, None, None),
        P(("grp", "view"), None),
        P("grp", None),
        P("view"),
    )
    out_specs = (P("view", "grp", None), P("grp", None))
    return jax.shard_map(
        per_device, mesh=mesh, in_specs=in_specs, out_specs=out_specs, check_vma=False
    )
```

```python
import functools

import jax
import jax.numpy as jnp
from jax import lax
from jax.experimental import pallas as pl
from jax.experimental.pallas import tpu as pltpu
from jax.sharding import PartitionSpec as P

ITERS = 4
LANES = 128
GROUP = 8


def each(start, end, body):
    if end - start < 16:
        for k in range(start, end):
            body(k)
        return

    def step(k, carry):
        body(k)
        return carry

    lax.fori_loop(start, end, step, 0)


def portions(n):
    ends = [n * part // 16 for part in (5, 12, 16)]
    starts = [0] + ends[:-1]
    return [(a, b) for a, b in zip(starts, ends) if b > a]


def kernel(
    n, feat_ref, off_ref, conf_ref, depth_ref, out_ref,
    feat, xs, xr, aux, deps, offv, offs, table, acc, sqs, picks, hots, part, costq, halves, summed, costs, rateq, rates, depcol, vs,
    local_sem, xs_send, xs_recv, aux_send, aux_recv, d_send, d_recv, h_send, h_recv, c_send, c_recv, v_send, v_recv,
):
    _, chans, rows, width = feat_ref.shape
    planes = off_ref.shape[-1]
    owned = depth_ref.shape[0]
    groups = n // rows
    cg = chans // groups
    pad = width // 8
    halo = ITERS
    pix = width // n
    step = max(GROUP, pix)
    span = step + 2 * halo
    per_window = step // pix
    lanes_out = vs.shape[-1]
    chunks = width // LANES
    entry_rows = chunks * cg
    me = lax.axis_index("view")
    my_row, my_group = me // groups, lax.rem(me, groups)
    reach = halves.shape[1]

    def block_of(device):
        return lax.rem(device, groups) * rows + device // groups

    my_block = block_of(me)

    lane = lax.broadcasted_iota(jnp.int32, (cg, LANES), 1)

    def build(place, x):
        pieces = [x[:, c * LANES:(c + 1) * LANES] for c in range(chunks)]
        for o in range(pad):
            turned = [pltpu.roll(piece, o, 1) if o else piece for piece in pieces]
            for c in range(chunks):
                before = turned[c - 1] if c else jnp.zeros_like(turned[c])
                line = jnp.where(lane >= o, turned[c], before) if o else turned[c]
                table[place * pad + o, c * cg:(c + 1) * cg, :] = line
        sqs[pl.ds(place, 1), :] = jnp.sum(x * x, axis=0, keepdims=True)

    barrier = pltpu.get_barrier_semaphore()

    def greet(k, carry):
        pl.semaphore_signal(barrier, inc=1, device_id={"view": lax.rem(me + k, n)})
        return carry

    lax.fori_loop(1, n, greet, 0)
    fetch = pltpu.make_async_copy(feat_ref.at[0], feat, local_sem)
    fetch.start()
    plane_lane = lax.broadcasted_iota(jnp.int32, (1, planes), 1)
    depth_row = jnp.zeros((1, planes), jnp.float32)
    for i in range(owned):
        depth_row = jnp.where(plane_lane == me * owned + i, depth_ref[i], depth_row)
    aux[me] = off_ref[...]
    deps[me] = depth_row
    fetch.wait()
    for r in range(rows):
        line = feat[:, r, :]
        for g in range(groups):
            xs[r * groups + g] = line[g * cg:(g + 1) * cg]
    pl.semaphore_wait(barrier, n - 1)

    def aux_copy(slot, peer):
        return pltpu.make_async_remote_copy(
            src_ref=aux.at[slot], dst_ref=aux.at[slot], send_sem=aux_send.at[peer],
            recv_sem=aux_recv.at[slot], device_id={"view": peer})

    def dep_copy(slot, peer):
        return pltpu.make_async_remote_copy(
            src_ref=deps.at[slot], dst_ref=deps.at[slot], send_sem=d_send.at[peer],
            recv_sem=d_recv.at[slot], device_id={"view": peer})

    def feat_copy(slot, peer):
        return pltpu.make_async_remote_copy(
            src_ref=xs.at[peer], dst_ref=xr.at[slot], send_sem=xs_send.at[peer],
            recv_sem=xs_recv.at[slot], device_id={"view": peer})

    each(1, n, lambda k: aux_copy(me, lax.rem(me + k, n)).start())
    each(1, n, lambda k: feat_copy(me, lax.rem(me + k, n)).start())
    each(1, n, lambda k: dep_copy(me, lax.rem(me + k, n)).start())
    build(0, xs[me])

    conf = (conf_ref[...].astype(jnp.float32) + 1.0) * 0.25
    rate = 0.15 * conf
    rate = jnp.concatenate([rate, jnp.zeros((LANES - rows, width), jnp.float32)], axis=0)
    rateq[...] = jnp.zeros_like(rateq)
    rateq[halo:halo + width, :] = rate.T
    first_pixel = pl.multiple_of(my_block // per_window * step, GROUP)
    near = rateq[pl.ds(first_pixel, span), :]
    for r in range(rows):
        rates[r] = jnp.broadcast_to(near[:, r:r + 1], (span, planes))
    costq[0:GROUP, :] = jnp.zeros((GROUP, planes), jnp.float32)
    costq[width:width + 2 * halo, :] = jnp.zeros((2 * halo, planes), jnp.float32)
    part[...] = jnp.zeros_like(part)

    shift = lax.broadcasted_iota(jnp.int32, (pad, width), 0)
    inside = lax.broadcasted_iota(jnp.int32, (pad, width), 1) >= shift

    per_hot = LANES // pad

    def squares(h):
        lines = []
        for k in range(h * per_hot, (h + 1) * per_hot):
            line = jnp.broadcast_to(sqs[k:k + 1, :], (pad, width))
            line = pltpu.roll(line, 0, 1, stride=1, stride_axis=0)
            lines.append(jnp.where(inside, line, 0.0))
        sq_all = jnp.concatenate(lines, axis=0)
        high = sq_all.astype(jnp.bfloat16)
        rest = sq_all - high.astype(jnp.float32)
        mid = rest.astype(jnp.bfloat16)
        low = (rest - mid.astype(jnp.float32)).astype(jnp.bfloat16)
        square = jnp.zeros((planes, width), jnp.float32)
        for piece in (low, mid, high):
            square = square + jnp.dot(hots[h], piece, preferred_element_type=jnp.float32)
        part[...] += square * (1.0 / (n * chans))

    def accumulate(start, end, is_last):
        def body(j, carry):
            sums = []
            for i in range(GROUP):
                p = j * GROUP + i
                total = acc[p] if start else None
                for k in range(start, end):
                    entry = table[offs[k, p]]
                    total = entry if total is None else total + entry
                if is_last:
                    total = total * total
                    sums.append(jnp.concatenate(
                        [jnp.sum(total[c * cg:(c + 1) * cg], axis=0, keepdims=True) for c in range(chunks)],
                        axis=1))
                else:
                    acc[p] = total
            if is_last:
                first = pl.multiple_of(j * GROUP, GROUP)
                part[pl.ds(first, GROUP), :] = (
                    part[pl.ds(first, GROUP), :]
                    - jnp.concatenate(sums, axis=0) * (1.0 / (n * n * chans)))
            return carry

        lax.fori_loop(0, planes // GROUP, body, 0)

    def take_offsets():
        each(1, n, lambda k: aux_copy(lax.rem(me - k + n, n), lax.rem(me - k + n, n)).wait_recv())
        for k in range(n):
            picks[k:k + 1, :] = aux[lax.rem(me - k + n, n)]
        places = lax.broadcasted_iota(jnp.int32, (n, planes), 0)
        offv[...] = picks[...] + places * pad
        to_scalar = pltpu.make_async_copy(offv, offs, local_sem)
        to_scalar.start()
        amount = lax.broadcasted_iota(jnp.int32, (pad, planes), 0)
        for h in range(n // per_hot):
            hot = jnp.concatenate(
                [jnp.where(picks[k:k + 1, :] == amount, 1.0, 0.0)
                 for k in range(h * per_hot, (h + 1) * per_hot)], axis=0)
            hots[h] = hot.T.astype(jnp.bfloat16)
        to_scalar.wait()

    done = 0
    for start, end in portions(n):
        first = max(start, 1)

        def receive(k, count):
            sources = [lax.rem(me - k - i + n, n) for i in range(count)]
            for source in sources:
                feat_copy(source, source).wait_recv()
            for i, source in enumerate(sources):
                build(k + i, xr[source])

        def receive_two(i, carry):
            receive(first + 2 * i, 2)
            return carry

        lax.fori_loop(0, (end - first) // 2, receive_two, 0)
        if (end - first) % 2:
            receive(end - 1, 1)
        if start == 0:
            take_offsets()
        while (done + 1) * per_hot <= end:
            squares(done)
            done += 1
        accumulate(start, end, end == n)

    costq[halo:halo + width, :] = part[...].T

    def reach_of(group):
        return pl.ds(pl.multiple_of(group * (rows // per_window) * step, GROUP), reach)

    def half_copy(slot, group):
        return pltpu.make_async_remote_copy(
            src_ref=costq.at[reach_of(group)], dst_ref=halves.at[slot],
            send_sem=h_send.at[group], recv_sem=h_recv.at[slot],
            device_id={"view": my_row * groups + group})

    each(1, groups, lambda k: half_copy(my_group, lax.rem(my_group + k, groups)).start())
    summed[...] = costq[reach_of(my_group), :]

    def add_half(k):
        source = lax.rem(my_group - k + groups, groups)
        half_copy(source, source).wait_recv()
        summed[...] += halves[source]

    each(1, groups, add_half)

    def cost_copy(slot, row):
        first = pl.multiple_of(row // per_window * step, GROUP)
        return pltpu.make_async_remote_copy(
            src_ref=summed.at[pl.ds(first, span)], dst_ref=costs.at[slot],
            send_sem=c_send.at[row], recv_sem=c_recv.at[slot],
            device_id={"view": row * groups + my_group})

    each(1, rows, lambda k: cost_copy(my_row, lax.rem(my_row + k, rows)).start())
    each(1, n, lambda k: dep_copy(lax.rem(me - k + n, n), lax.rem(me - k + n, n)).wait_recv())
    all_depths = jnp.sum(deps[:, 0, :], axis=0, keepdims=True)
    depcol[...] = jnp.broadcast_to(all_depths, (lanes_out, planes)).T
    costs[my_row] = summed[pl.ds(pl.multiple_of(my_row // per_window * step, GROUP), span), :]

    each(1, rows, lambda k: cost_copy(lax.rem(my_row - k + rows, rows), lax.rem(my_row - k + rows, rows)).wait_recv())

    plane = lax.broadcasted_iota(jnp.int32, (span, planes), 1)
    cost = [costs[r] for r in range(rows)]
    for _ in range(ITERS):
        new = []
        for r in range(rows):
            c = cost[r]
            beside = pltpu.roll(c, 1, 0) + pltpu.roll(c, span - 1, 0)
            if r > 0:
                beside = beside + cost[r - 1]
            if r < rows - 1:
                beside = beside + cost[r + 1]
            beside = beside + jnp.where(plane > 0, pltpu.roll(c, 1, 1), 0.0)
            beside = beside + jnp.where(plane < planes - 1, pltpu.roll(c, planes - 1, 1), 0.0)
            new.append(c + rates[r] * (beside - 6.0 * c))
        cost = new

    mine = []
    for r in range(rows):
        own = cost[r][halo:halo + pix]
        for m in range(1, per_window):
            first = halo + m * pix
            own = jnp.where(lax.rem(my_block, per_window) == m, cost[r][first:first + pix], own)
        mine.append(own)
    if lanes_out > rows * pix:
        mine.append(jnp.zeros((lanes_out - rows * pix, planes), jnp.float32))
    final = jnp.concatenate(mine, axis=0).T
    peak = jnp.max(-final, axis=0, keepdims=True)
    weight = jnp.exp(-final - peak)
    denom = jnp.sum(weight, axis=0, keepdims=True)
    numer = jnp.sum(weight * depcol[...], axis=0, keepdims=True)
    depth = numer / denom
    for j in range(n):
        vs[j, 0:owned, :] = final[j * owned:(j + 1) * owned]
        vs[j, owned:owned + 1, :] = depth

    def out_copy(slot, peer):
        return pltpu.make_async_remote_copy(
            src_ref=vs.at[peer], dst_ref=out_ref.at[slot],
            send_sem=v_send.at[peer], recv_sem=v_recv.at[slot], device_id={"view": peer})

    each(1, n, lambda k: out_copy(my_block, lax.rem(me + k, n)).start())
    out_ref[my_block] = vs[me]

    def finish(k, carry):
        peer = lax.rem(me + k, n)
        aux_copy(me, peer).wait_send()
        dep_copy(me, peer).wait_send()
        feat_copy(me, peer).wait_send()
        return carry

    lax.fori_loop(1, n, finish, 0)
    each(1, groups, lambda k: half_copy(my_group, lax.rem(my_group + k, groups)).wait_send())
    each(1, rows, lambda k: cost_copy(my_row, lax.rem(my_row + k, rows)).wait_send())

    each(1, n, lambda k: out_copy(block_of(lax.rem(me - k + n, n)), lax.rem(me - k + n, n)).wait_recv())
    each(1, n, lambda k: out_copy(my_block, lax.rem(me + k, n)).wait_send())


def lay_out(pieces, cost_out, map_out):
    n = pieces.shape[0]
    owned, rows, width = cost_out.shape
    pix = width // n
    per_chunk = LANES // pix
    lane = lax.broadcasted_iota(jnp.int32, (owned + 1, LANES), 1) // pix
    for c in range(width // LANES):
        for r in range(rows):
            line = None
            for k in range(per_chunk):
                piece = pieces[c * per_chunk + k]
                shift = (k - r) * pix % LANES
                if shift:
                    piece = pltpu.roll(piece, shift, 1)
                line = piece if line is None else jnp.where(lane == k, piece, line)
            cost_out[:, r, c * LANES:(c + 1) * LANES] = line[:owned]
            map_out[r:r + 1, c * LANES:(c + 1) * LANES] = line[owned:]


def per_device(features, offsets, conf_bins, plane_depths):
    n = lax.axis_size("view")
    _, chans, rows, width = features.shape
    planes = offsets.shape[-1]
    owned = plane_depths.shape[0]
    cg = chans * rows // n
    pad = width // 8
    pix = width // n
    groups = n // rows
    step = max(GROUP, pix)
    span = step + 2 * ITERS
    reach = (rows * pix // step - 1) * step + span
    lanes_out = max(LANES, rows * pix)
    f32 = jnp.float32
    vmem = pl.BlockSpec(memory_space=pltpu.VMEM)
    dma = pltpu.SemaphoreType.DMA
    pieces = pl.pallas_call(
        functools.partial(kernel, n),
        out_shape=jax.ShapeDtypeStruct((n, owned + 1, lanes_out), f32),
        in_specs=[pl.BlockSpec(memory_space=pl.ANY), vmem, vmem, pl.BlockSpec(memory_space=pltpu.SMEM)],
        out_specs=vmem,
        scratch_shapes=[
            pltpu.VMEM((chans, rows, width), f32),
            pltpu.VMEM((n, cg, width), f32),
            pltpu.VMEM((n, cg, width), f32),
            pltpu.VMEM((n, 1, planes), jnp.int32),
            pltpu.VMEM((n, 1, planes), f32),
            pltpu.VMEM((n, planes), jnp.int32),
            pltpu.SMEM((n, planes), jnp.int32),
            pltpu.VMEM((n * pad, cg * width // LANES, LANES), f32),
            pltpu.VMEM((planes, cg * width // LANES, LANES), f32),
            pltpu.VMEM((n, width), f32),
            pltpu.VMEM((n, planes), jnp.int32),
            pltpu.VMEM((n * pad // LANES, planes, LANES), jnp.bfloat16),
            pltpu.VMEM((planes, width), f32),
            pltpu.VMEM((width + 2 * ITERS, planes), f32),
            pltpu.VMEM((groups, reach, planes), f32),
            pltpu.VMEM((reach, planes), f32),
            pltpu.VMEM((rows, span, planes), f32),
            pltpu.VMEM((width + 2 * ITERS, LANES), f32),
            pltpu.VMEM((rows, span, planes), f32),
            pltpu.VMEM((planes, lanes_out), f32),
            pltpu.VMEM((n, owned + 1, lanes_out), f32),
            dma,
        ] + [dma((n,)) for _ in range(6)] + [dma((groups,))] * 2 + [dma((rows,))] * 2 + [dma((n,))] * 2,
        compiler_params=pltpu.CompilerParams(collective_id=0, has_side_effects=True,
                                             vmem_limit_bytes=60 << 20),
    )(features, offsets, conf_bins, plane_depths)
    return pl.pallas_call(
        lay_out,
        out_shape=(
            jax.ShapeDtypeStruct((owned, rows, width), f32),
            jax.ShapeDtypeStruct((rows, width), f32),
        ),
        in_specs=[vmem],
        out_specs=(vmem, vmem),
    )(pieces)


def solution(mesh):
    in_specs = (
        P(("grp", "view"), None, None, None),
        P(("grp", "view"), None),
        P("grp", None),
        P("view"),
    )
    out_specs = (P("view", "grp", None), P("grp", None))
    return jax.shard_map(
        per_device, mesh=mesh, in_specs=in_specs, out_specs=out_specs, check_vma=False
    )
```

```python
import functools

import jax
import jax.numpy as jnp
from jax import lax
from jax.experimental import pallas as pl
from jax.experimental.pallas import tpu as pltpu
from jax.sharding import PartitionSpec as P

ITERS = 4
LANES = 128
GROUP = 8


def each(start, end, body):
    if end - start < 16:
        for k in range(start, end):
            body(k)
        return

    def step(k, carry):
        body(k)
        return carry

    lax.fori_loop(start, end, step, 0)


def portions(n):
    ends = [n * part // 16 for part in (6, 13, 16)]
    starts = [0] + ends[:-1]
    return [(a, b) for a, b in zip(starts, ends) if b > a]


def kernel(
    n, feat_ref, off_ref, conf_ref, depth_ref, out_ref,
    feat, xs, xr, aux, deps, offv, offs, table, acc, sqs, picks, hots, part, costq, halves, summed, costs, rateq, rates, depcol, vs,
    local_sem, o_sem, xs_send, xs_recv, aux_send, aux_recv, d_send, d_recv, h_send, h_recv, c_send, c_recv, v_send, v_recv,
):
    _, chans, rows, width = feat_ref.shape
    planes = off_ref.shape[-1]
    owned = depth_ref.shape[0]
    groups = n // rows
    cg = chans // groups
    pad = width // 8
    halo = ITERS
    pix = width // n
    step = max(GROUP, pix)
    span = step + 2 * halo
    per_window = step // pix
    lanes_out = vs.shape[-1]
    chunks = width // LANES
    entry_rows = chunks * cg
    me = lax.axis_index("view")
    my_row, my_group = me // groups, lax.rem(me, groups)
    reach = halves.shape[1]

    def block_of(device):
        return lax.rem(device, groups) * rows + device // groups

    my_block = block_of(me)

    lane = lax.broadcasted_iota(jnp.int32, (cg, LANES), 1)

    def build(place, x):
        pieces = [x[:, c * LANES:(c + 1) * LANES] for c in range(chunks)]
        for o in range(pad):
            turned = [pltpu.roll(piece, o, 1) if o else piece for piece in pieces]
            for c in range(chunks):
                before = turned[c - 1] if c else jnp.zeros_like(turned[c])
                line = jnp.where(lane >= o, turned[c], before) if o else turned[c]
                first = pl.multiple_of(place * pad * entry_rows, GROUP) + o * entry_rows + c * cg
                table[pl.ds(first, cg), :] = line
        sqs[pl.ds(place, 1), :] = jnp.sum(x * x, axis=0, keepdims=True)

    barrier = pltpu.get_barrier_semaphore()

    def greet(k, carry):
        pl.semaphore_signal(barrier, inc=1, device_id={"view": lax.rem(me + k, n)})
        return carry

    lax.fori_loop(1, n, greet, 0)
    fetch = pltpu.make_async_copy(feat_ref.at[0], feat, local_sem)
    fetch.start()
    plane_lane = lax.broadcasted_iota(jnp.int32, (1, planes), 1)
    depth_row = jnp.zeros((1, planes), jnp.float32)
    for i in range(owned):
        depth_row = jnp.where(plane_lane == me * owned + i, depth_ref[i], depth_row)
    aux[me] = off_ref[...]
    deps[me] = depth_row
    fetch.wait()
    for r in range(rows):
        line = feat[:, r, :]
        for g in range(groups):
            xs[r * groups + g] = line[g * cg:(g + 1) * cg]
    pl.semaphore_wait(barrier, n - 1)

    def aux_copy(slot, peer):
        return pltpu.make_async_remote_copy(
            src_ref=aux.at[slot], dst_ref=aux.at[slot], send_sem=aux_send.at[peer],
            recv_sem=aux_recv.at[slot], device_id={"view": peer})

    def dep_copy(slot, peer):
        return pltpu.make_async_remote_copy(
            src_ref=deps.at[slot], dst_ref=deps.at[slot], send_sem=d_send.at[peer],
            recv_sem=d_recv.at[slot], device_id={"view": peer})

    def feat_copy(slot, peer):
        return pltpu.make_async_remote_copy(
            src_ref=xs.at[peer], dst_ref=xr.at[slot], send_sem=xs_send.at[peer],
            recv_sem=xs_recv.at[slot], device_id={"view": peer})

    each(1, n, lambda k: aux_copy(me, lax.rem(me + k, n)).start())
    each(1, n, lambda k: feat_copy(me, lax.rem(me + k, n)).start())
    each(1, n, lambda k: dep_copy(me, lax.rem(me + k, n)).start())
    build(0, xs[me])

    conf = (conf_ref[...].astype(jnp.float32) + 1.0) * 0.25
    rate = 0.15 * conf
    rate = jnp.concatenate([rate, jnp.zeros((LANES - rows, width), jnp.float32)], axis=0)
    rateq[...] = jnp.zeros_like(rateq)
    rateq[halo:halo + width, :] = rate.T
    first_pixel = pl.multiple_of(my_block // per_window * step, GROUP)
    near = rateq[pl.ds(first_pixel, span), :]
    for r in range(rows):
        rates[r] = jnp.broadcast_to(near[:, r:r + 1], (span, planes))
    costq[0:GROUP, :] = jnp.zeros((GROUP, planes), jnp.float32)
    costq[width:width + 2 * halo, :] = jnp.zeros((2 * halo, planes), jnp.float32)
    part[...] = jnp.zeros_like(part)

    shift = lax.broadcasted_iota(jnp.int32, (pad, width), 0)
    inside = lax.broadcasted_iota(jnp.int32, (pad, width), 1) >= shift

    per_hot = LANES // pad

    def squares(h):
        lines = []
        for k in range(h * per_hot, (h + 1) * per_hot):
            line = jnp.broadcast_to(sqs[k:k + 1, :], (pad, width))
            line = pltpu.roll(line, 0, 1, stride=1, stride_axis=0)
            lines.append(jnp.where(inside, line, 0.0))
        sq_all = jnp.concatenate(lines, axis=0)
        high = sq_all.astype(jnp.bfloat16)
        rest = sq_all - high.astype(jnp.float32)
        mid = rest.astype(jnp.bfloat16)
        low = (rest - mid.astype(jnp.float32)).astype(jnp.bfloat16)
        square = jnp.zeros((planes, width), jnp.float32)
        for piece in (low, mid, high):
            square = square + jnp.dot(hots[h], piece, preferred_element_type=jnp.float32)
        part[...] += square * (1.0 / (n * chans))

    def accumulate(start, end, is_last):
        def body(j, carry):
            sums = []
            for i in range(GROUP):
                p = j * GROUP + i
                total = acc[p] if start else None
                for k in range(start, end):
                    entry = table[pl.ds(offs[k][0, p], entry_rows), :]
                    total = entry if total is None else total + entry
                if is_last:
                    total = total * total
                    sums.append(jnp.concatenate(
                        [jnp.sum(total[c * cg:(c + 1) * cg], axis=0, keepdims=True) for c in range(chunks)],
                        axis=1))
                else:
                    acc[p] = total
            if is_last:
                first = pl.multiple_of(j * GROUP, GROUP)
                part[pl.ds(first, GROUP), :] = (
                    part[pl.ds(first, GROUP), :]
                    - jnp.concatenate(sums, axis=0) * (1.0 / (n * n * chans)))
            return carry

        def body_two(j, carry):
            return body(2 * j + 1, body(2 * j, carry))

        lax.fori_loop(0, planes // GROUP // 2, body_two, 0)

    def take_offsets():
        each(1, n, lambda k: aux_copy(lax.rem(me - k + n, n), lax.rem(me - k + n, n)).wait_recv())
        for k in range(n):
            picks[k:k + 1, :] = aux[lax.rem(me - k + n, n)]
        places = lax.broadcasted_iota(jnp.int32, (n, planes), 0)
        offv[:, 0, :] = (picks[...] + places * pad) * entry_rows
        to_scalar = [pltpu.make_async_copy(offv.at[k], offs[k], o_sem.at[k]) for k in range(n)]
        for copy in to_scalar:
            copy.start()
        amount = lax.broadcasted_iota(jnp.int32, (pad, planes), 0)
        for h in range(n // per_hot):
            hot = jnp.concatenate(
                [jnp.where(picks[k:k + 1, :] == amount, 1.0, 0.0)
                 for k in range(h * per_hot, (h + 1) * per_hot)], axis=0)
            hots[h] = hot.T.astype(jnp.bfloat16)
        for copy in to_scalar:
            copy.wait()

    done = 0
    for start, end in portions(n):
        first = max(start, 1)

        def receive(k, count):
            sources = [lax.rem(me - k - i + n, n) for i in range(count)]
            for source in sources:
                feat_copy(source, source).wait_recv()
            for i, source in enumerate(sources):
                build(k + i, xr[source])

        def receive_two(i, carry):
            receive(first + 2 * i, 2)
            return carry

        lax.fori_loop(0, (end - first) // 2, receive_two, 0)
        if (end - first) % 2:
            receive(end - 1, 1)
        if start == 0:
            take_offsets()
        while (done + 1) * per_hot <= end:
            squares(done)
            done += 1
        accumulate(start, end, end == n)

    costq[halo:halo + width, :] = part[...].T

    def reach_of(group):
        return pl.ds(pl.multiple_of(group * (rows // per_window) * step, GROUP), reach)

    def half_copy(slot, group):
        return pltpu.make_async_remote_copy(
            src_ref=costq.at[reach_of(group)], dst_ref=halves.at[slot],
            send_sem=h_send.at[group], recv_sem=h_recv.at[slot],
            device_id={"view": my_row * groups + group})

    each(1, groups, lambda k: half_copy(my_group, lax.rem(my_group + k, groups)).start())
    summed[...] = costq[reach_of(my_group), :]

    def add_half(k):
        source = lax.rem(my_group - k + groups, groups)
        half_copy(source, source).wait_recv()
        summed[...] += halves[source]

    each(1, groups, add_half)

    def cost_copy(slot, row):
        first = pl.multiple_of(row // per_window * step, GROUP)
        return pltpu.make_async_remote_copy(
            src_ref=summed.at[pl.ds(first, span)], dst_ref=costs.at[slot],
            send_sem=c_send.at[row], recv_sem=c_recv.at[slot],
            device_id={"view": row * groups + my_group})

    each(1, rows, lambda k: cost_copy(my_row, lax.rem(my_row + k, rows)).start())
    each(1, n, lambda k: dep_copy(lax.rem(me - k + n, n), lax.rem(me - k + n, n)).wait_recv())
    all_depths = jnp.sum(deps[:, 0, :], axis=0, keepdims=True)
    depcol[...] = jnp.broadcast_to(all_depths, (lanes_out, planes)).T
    costs[my_row] = summed[pl.ds(pl.multiple_of(my_row // per_window * step, GROUP), span), :]

    each(1, rows, lambda k: cost_copy(lax.rem(my_row - k + rows, rows), lax.rem(my_row - k + rows, rows)).wait_recv())

    plane = lax.broadcasted_iota(jnp.int32, (span, planes), 1)
    cost = [costs[r] for r in range(rows)]
    for _ in range(ITERS):
        new = []
        for r in range(rows):
            c = cost[r]
            beside = pltpu.roll(c, 1, 0) + pltpu.roll(c, span - 1, 0)
            if r > 0:
                beside = beside + cost[r - 1]
            if r < rows - 1:
                beside = beside + cost[r + 1]
            beside = beside + jnp.where(plane > 0, pltpu.roll(c, 1, 1), 0.0)
            beside = beside + jnp.where(plane < planes - 1, pltpu.roll(c, planes - 1, 1), 0.0)
            new.append(c + rates[r] * (beside - 6.0 * c))
        cost = new

    mine = []
    for r in range(rows):
        own = cost[r][halo:halo + pix]
        for m in range(1, per_window):
            first = halo + m * pix
            own = jnp.where(lax.rem(my_block, per_window) == m, cost[r][first:first + pix], own)
        mine.append(own)
    if lanes_out > rows * pix:
        mine.append(jnp.zeros((lanes_out - rows * pix, planes), jnp.float32))
    final = jnp.concatenate(mine, axis=0).T
    peak = jnp.max(-final, axis=0, keepdims=True)
    weight = jnp.exp(-final - peak)
    denom = jnp.sum(weight, axis=0, keepdims=True)
    numer = jnp.sum(weight * depcol[...], axis=0, keepdims=True)
    depth = numer / denom
    for j in range(n):
        vs[j, 0:owned, :] = final[j * owned:(j + 1) * owned]
        vs[j, owned:owned + 1, :] = depth

    def out_copy(slot, peer):
        return pltpu.make_async_remote_copy(
            src_ref=vs.at[peer], dst_ref=out_ref.at[slot],
            send_sem=v_send.at[peer], recv_sem=v_recv.at[slot], device_id={"view": peer})

    each(1, n, lambda k: out_copy(my_block, lax.rem(me + k, n)).start())
    out_ref[my_block] = vs[me]

    def finish(k, carry):
        peer = lax.rem(me + k, n)
        aux_copy(me, peer).wait_send()
        dep_copy(me, peer).wait_send()
        feat_copy(me, peer).wait_send()
        return carry

    lax.fori_loop(1, n, finish, 0)
    each(1, groups, lambda k: half_copy(my_group, lax.rem(my_group + k, groups)).wait_send())
    each(1, rows, lambda k: cost_copy(my_row, lax.rem(my_row + k, rows)).wait_send())

    each(1, n, lambda k: out_copy(block_of(lax.rem(me - k + n, n)), lax.rem(me - k + n, n)).wait_recv())
    each(1, n, lambda k: out_copy(my_block, lax.rem(me + k, n)).wait_send())


def lay_out(pieces, cost_out, map_out):
    n = pieces.shape[0]
    owned, rows, width = cost_out.shape
    pix = width // n
    per_chunk = LANES // pix
    for c in range(width // LANES):
        at = slice(c * LANES, (c + 1) * LANES)
        if per_chunk == rows == GROUP:
            blocks = [pieces[c * rows + k, 0:owned, :] for k in range(rows)]
            lane = lax.broadcasted_iota(jnp.int32, (owned, LANES), 1) // pix
            for d in (4, 2, 1):
                upper = lax.rem(lane // d, 2) == 1
                for k in range(rows):
                    if k & d == 0:
                        a, b = blocks[k], blocks[k + d]
                        blocks[k] = jnp.where(upper, pltpu.roll(b, d * pix, 1), a)
                        blocks[k + d] = jnp.where(upper, b, pltpu.roll(a, LANES - d * pix, 1))
            for r in range(rows):
                cost_out[:, r, at] = blocks[r]
            depths = jnp.concatenate([pieces[c * rows + k, owned:, :] for k in range(rows)], axis=0)
            lane = lax.broadcasted_iota(jnp.int32, (rows, LANES), 1) // pix
            apart = lane - lax.broadcasted_iota(jnp.int32, (rows, LANES), 0)
            line = depths
            for d in range(1, rows):
                moved = pltpu.roll(pltpu.roll(depths, d * pix, 1), rows - d, 0)
                line = jnp.where(jnp.logical_or(apart == d, apart == d - rows), moved, line)
            map_out[:, at] = line
            continue
        lane = lax.broadcasted_iota(jnp.int32, (owned + 1, LANES), 1) // pix
        for r in range(rows):
            line = None
            for k in range(per_chunk):
                piece = pieces[c * per_chunk + k]
                shift = (k - r) * pix % LANES
                if shift:
                    piece = pltpu.roll(piece, shift, 1)
                line = piece if line is None else jnp.where(lane == k, piece, line)
            cost_out[:, r, at] = line[:owned]
            map_out[r:r + 1, at] = line[owned:]


def per_device(features, offsets, conf_bins, plane_depths):
    n = lax.axis_size("view")
    _, chans, rows, width = features.shape
    planes = offsets.shape[-1]
    owned = plane_depths.shape[0]
    cg = chans * rows // n
    pad = width // 8
    pix = width // n
    groups = n // rows
    step = max(GROUP, pix)
    span = step + 2 * ITERS
    reach = (rows * pix // step - 1) * step + span
    lanes_out = max(LANES, rows * pix)
    f32 = jnp.float32
    vmem = pl.BlockSpec(memory_space=pltpu.VMEM)
    dma = pltpu.SemaphoreType.DMA
    pieces = pl.pallas_call(
        functools.partial(kernel, n),
        out_shape=jax.ShapeDtypeStruct((n, owned + 1, lanes_out), f32),
        in_specs=[pl.BlockSpec(memory_space=pl.ANY), vmem, vmem, pl.BlockSpec(memory_space=pltpu.SMEM)],
        out_specs=vmem,
        scratch_shapes=[
            pltpu.VMEM((chans, rows, width), f32),
            pltpu.VMEM((n, cg, width), f32),
            pltpu.VMEM((n, cg, width), f32),
            pltpu.VMEM((n, 1, planes), jnp.int32),
            pltpu.VMEM((n, 1, planes), f32),
            pltpu.VMEM((n, 1, planes), jnp.int32),
            tuple(pltpu.SMEM((1, planes), jnp.int32) for _ in range(n)),
            pltpu.VMEM((n * pad * cg * width // LANES, LANES), f32),
            pltpu.VMEM((planes, cg * width // LANES, LANES), f32),
            pltpu.VMEM((n, width), f32),
            pltpu.VMEM((n, planes), jnp.int32),
            pltpu.VMEM((n * pad // LANES, planes, LANES), jnp.bfloat16),
            pltpu.VMEM((planes, width), f32),
            pltpu.VMEM((width + 2 * ITERS, planes), f32),
            pltpu.VMEM((groups, reach, planes), f32),
            pltpu.VMEM((reach, planes), f32),
            pltpu.VMEM((rows, span, planes), f32),
            pltpu.VMEM((width + 2 * ITERS, LANES), f32),
            pltpu.VMEM((rows, span, planes), f32),
            pltpu.VMEM((planes, lanes_out), f32),
            pltpu.VMEM((n, owned + 1, lanes_out), f32),
            dma,
        ] + [dma((n,)) for _ in range(7)] + [dma((groups,))] * 2 + [dma((rows,))] * 2 + [dma((n,))] * 2,
        compiler_params=pltpu.CompilerParams(collective_id=0, has_side_effects=True,
                                             vmem_limit_bytes=60 << 20),
    )(features, offsets, conf_bins, plane_depths)
    return pl.pallas_call(
        lay_out,
        out_shape=(
            jax.ShapeDtypeStruct((owned, rows, width), f32),
            jax.ShapeDtypeStruct((rows, width), f32),
        ),
        in_specs=[vmem],
        out_specs=(vmem, vmem),
    )(pieces)


def solution(mesh):
    in_specs = (
        P(("grp", "view"), None, None, None),
        P(("grp", "view"), None),
        P("grp", None),
        P("view"),
    )
    out_specs = (P("view", "grp", None), P("grp", None))
    return jax.shard_map(
        per_device, mesh=mesh, in_specs=in_specs, out_specs=out_specs, check_vma=False
    )
```

```python
import functools

import jax
import jax.numpy as jnp
from jax import lax
from jax.experimental import pallas as pl
from jax.experimental.pallas import tpu as pltpu
from jax.sharding import PartitionSpec as P

ITERS = 4
LANES = 128
GROUP = 8


def each(start, end, body):
    if end - start < 16:
        for k in range(start, end):
            body(k)
        return

    def step(k, carry):
        body(k)
        return carry

    lax.fori_loop(start, end, step, 0)


def portions(n):
    ends = [n * part // 16 for part in (6, 13, 16)]
    starts = [0] + ends[:-1]
    return [(a, b) for a, b in zip(starts, ends) if b > a]


def kernel(
    n, feat_ref, off_ref, conf_ref, depth_ref, out_ref,
    feat, xs, xr, aux, deps, offv, offs, table, acc, sqs, picks, hots, part, costq, halves, summed, costs, rateq, rates, depcol, vs,
    local_sem, o_sem, xs_send, xs_recv, aux_send, aux_recv, d_send, d_recv, h_send, h_recv, c_send, c_recv, v_send, v_recv,
):
    _, chans, rows, width = feat_ref.shape
    planes = off_ref.shape[-1]
    owned = depth_ref.shape[0]
    groups = n // rows
    cg = chans // groups
    pad = width // 8
    halo = ITERS
    pix = width // n
    step = max(GROUP, pix)
    span = step + 2 * halo
    per_window = step // pix
    lanes_out = vs.shape[-1]
    chunks = width // LANES
    entry_rows = chunks * cg
    me = lax.axis_index("view")
    my_row, my_group = me // groups, lax.rem(me, groups)
    reach = halves.shape[1]

    def block_of(device):
        return lax.rem(device, groups) * rows + device // groups

    my_block = block_of(me)

    lane = lax.broadcasted_iota(jnp.int32, (cg, LANES), 1)

    def build(place, x):
        pieces = [x[:, c * LANES:(c + 1) * LANES] for c in range(chunks)]
        for o in range(pad):
            turned = [pltpu.roll(piece, o, 1) if o else piece for piece in pieces]
            for c in range(chunks):
                before = turned[c - 1] if c else jnp.zeros_like(turned[c])
                line = jnp.where(lane >= o, turned[c], before) if o else turned[c]
                first = pl.multiple_of(place * pad * entry_rows, GROUP) + o * entry_rows + c * cg
                table[pl.ds(first, cg), :] = line
        sqs[pl.ds(place, 1), :] = jnp.sum(x * x, axis=0, keepdims=True)

    barrier = pltpu.get_barrier_semaphore()

    def greet(k, carry):
        pl.semaphore_signal(barrier, inc=1, device_id={"view": lax.rem(me + k, n)})
        return carry

    lax.fori_loop(1, n, greet, 0)
    fetch = pltpu.make_async_copy(feat_ref.at[0], feat, local_sem)
    fetch.start()
    plane_lane = lax.broadcasted_iota(jnp.int32, (1, planes), 1)
    depth_row = jnp.zeros((1, planes), jnp.float32)
    for i in range(owned):
        depth_row = jnp.where(plane_lane == me * owned + i, depth_ref[i], depth_row)
    aux[me] = off_ref[...]
    deps[me] = depth_row
    fetch.wait()
    for r in range(rows):
        line = feat[:, r, :]
        for g in range(groups):
            xs[r * groups + g] = line[g * cg:(g + 1) * cg]
    pl.semaphore_wait(barrier, n - 1)

    def aux_copy(slot, peer):
        return pltpu.make_async_remote_copy(
            src_ref=aux.at[slot], dst_ref=aux.at[slot], send_sem=aux_send.at[peer],
            recv_sem=aux_recv.at[slot], device_id={"view": peer})

    def dep_copy(slot, peer):
        return pltpu.make_async_remote_copy(
            src_ref=deps.at[slot], dst_ref=deps.at[slot], send_sem=d_send.at[peer],
            recv_sem=d_recv.at[slot], device_id={"view": peer})

    def feat_copy(slot, peer):
        return pltpu.make_async_remote_copy(
            src_ref=xs.at[peer], dst_ref=xr.at[slot], send_sem=xs_send.at[peer],
            recv_sem=xs_recv.at[slot], device_id={"view": peer})

    each(1, n, lambda k: aux_copy(me, lax.rem(me + k, n)).start())
    each(1, n, lambda k: feat_copy(me, lax.rem(me + k, n)).start())
    each(1, n, lambda k: dep_copy(me, lax.rem(me + k, n)).start())
    build(0, xs[me])

    conf = (conf_ref[...].astype(jnp.float32) + 1.0) * 0.25
    rate = 0.15 * conf
    rate = jnp.concatenate([rate, jnp.zeros((LANES - rows, width), jnp.float32)], axis=0)
    rateq[...] = jnp.zeros_like(rateq)
    rateq[halo:halo + width, :] = rate.T
    first_pixel = pl.multiple_of(my_block // per_window * step, GROUP)
    near = rateq[pl.ds(first_pixel, span), :]
    for r in range(rows):
        rates[r] = jnp.broadcast_to(near[:, r:r + 1], (span, planes))
    costq[0:GROUP, :] = jnp.zeros((GROUP, planes), jnp.float32)
    costq[width:width + 2 * halo, :] = jnp.zeros((2 * halo, planes), jnp.float32)
    part[...] = jnp.zeros_like(part)

    shift = lax.broadcasted_iota(jnp.int32, (pad, width), 0)
    inside = lax.broadcasted_iota(jnp.int32, (pad, width), 1) >= shift

    per_hot = LANES // pad

    def squares(h):
        lines = []
        for k in range(h * per_hot, (h + 1) * per_hot):
            line = jnp.broadcast_to(sqs[k:k + 1, :], (pad, width))
            line = pltpu.roll(line, 0, 1, stride=1, stride_axis=0)
            lines.append(jnp.where(inside, line, 0.0))
        sq_all = jnp.concatenate(lines, axis=0)
        high = sq_all.astype(jnp.bfloat16)
        rest = sq_all - high.astype(jnp.float32)
        mid = rest.astype(jnp.bfloat16)
        low = (rest - mid.astype(jnp.float32)).astype(jnp.bfloat16)
        square = jnp.zeros((planes, width), jnp.float32)
        for piece in (low, mid, high):
            square = square + jnp.dot(hots[h], piece, preferred_element_type=jnp.float32)
        part[...] += square * (1.0 / (n * chans))

    def accumulate(start, end, is_last):
        def body(j, carry):
            sums = []
            for i in range(GROUP):
                p = j * GROUP + i
                total = acc[p] if start else None
                for k in range(start, end):
                    entry = table[pl.ds(offs[k][0, p], entry_rows), :]
                    total = entry if total is None else total + entry
                if is_last:
                    total = total * total
                    sums.append(jnp.concatenate(
                        [jnp.sum(total[c * cg:(c + 1) * cg], axis=0, keepdims=True) for c in range(chunks)],
                        axis=1))
                else:
                    acc[p] = total
            if is_last:
                first = pl.multiple_of(j * GROUP, GROUP)
                part[pl.ds(first, GROUP), :] = (
                    part[pl.ds(first, GROUP), :]
                    - jnp.concatenate(sums, axis=0) * (1.0 / (n * n * chans)))
            return carry

        def body_two(j, carry):
            return body(2 * j + 1, body(2 * j, carry))

        lax.fori_loop(0, planes // GROUP // 2, body_two, 0)

    def take_offsets():
        each(1, n, lambda k: aux_copy(lax.rem(me - k + n, n), lax.rem(me - k + n, n)).wait_recv())
        for k in range(n):
            picks[k:k + 1, :] = aux[lax.rem(me - k + n, n)]
        places = lax.broadcasted_iota(jnp.int32, (n, planes), 0)
        offv[:, 0, :] = (picks[...] + places * pad) * entry_rows
        to_scalar = [pltpu.make_async_copy(offv.at[k], offs[k], o_sem.at[k]) for k in range(n)]
        for copy in to_scalar:
            copy.start()
        amount = lax.broadcasted_iota(jnp.int32, (pad, planes), 0)
        for h in range(n // per_hot):
            hot = jnp.concatenate(
                [jnp.where(picks[k:k + 1, :] == amount, 1.0, 0.0)
                 for k in range(h * per_hot, (h + 1) * per_hot)], axis=0)
            hots[h] = hot.T.astype(jnp.bfloat16)
        for copy in to_scalar:
            copy.wait()

    done = 0
    for start, end in portions(n):
        first = max(start, 1)

        def receive(k, count):
            sources = [lax.rem(me - k - i + n, n) for i in range(count)]
            for source in sources:
                feat_copy(source, source).wait_recv()
            for i, source in enumerate(sources):
                build(k + i, xr[source])

        batch = min(3, end - first)

        def receive_batch(i, carry):
            receive(first + batch * i, batch)
            return carry

        whole = (end - first) // batch
        lax.fori_loop(0, whole, receive_batch, 0)
        if (end - first) % batch:
            receive(first + whole * batch, (end - first) % batch)
        if start == 0:
            take_offsets()
        while (done + 1) * per_hot <= end:
            squares(done)
            done += 1
        accumulate(start, end, end == n)

    costq[halo:halo + width, :] = part[...].T

    def reach_of(group):
        return pl.ds(pl.multiple_of(group * (rows // per_window) * step, GROUP), reach)

    def half_copy(slot, group):
        return pltpu.make_async_remote_copy(
            src_ref=costq.at[reach_of(group)], dst_ref=halves.at[slot],
            send_sem=h_send.at[group], recv_sem=h_recv.at[slot],
            device_id={"view": my_row * groups + group})

    each(1, groups, lambda k: half_copy(my_group, lax.rem(my_group + k, groups)).start())
    summed[...] = costq[reach_of(my_group), :]

    def add_half(k):
        source = lax.rem(my_group - k + groups, groups)
        half_copy(source, source).wait_recv()
        summed[...] += halves[source]

    each(1, groups, add_half)

    def cost_copy(slot, row):
        first = pl.multiple_of(row // per_window * step, GROUP)
        return pltpu.make_async_remote_copy(
            src_ref=summed.at[pl.ds(first, span)], dst_ref=costs.at[slot],
            send_sem=c_send.at[row], recv_sem=c_recv.at[slot],
            device_id={"view": row * groups + my_group})

    each(1, rows, lambda k: cost_copy(my_row, lax.rem(my_row + k, rows)).start())
    each(1, n, lambda k: dep_copy(lax.rem(me - k + n, n), lax.rem(me - k + n, n)).wait_recv())
    all_depths = jnp.sum(deps[:, 0, :], axis=0, keepdims=True)
    depcol[...] = jnp.broadcast_to(all_depths, (lanes_out, planes)).T
    costs[my_row] = summed[pl.ds(pl.multiple_of(my_row // per_window * step, GROUP), span), :]

    each(1, rows, lambda k: cost_copy(lax.rem(my_row - k + rows, rows), lax.rem(my_row - k + rows, rows)).wait_recv())

    plane = lax.broadcasted_iota(jnp.int32, (span, planes), 1)
    cost = [costs[r] for r in range(rows)]
    for _ in range(ITERS):
        new = []
        for r in range(rows):
            c = cost[r]
            beside = pltpu.roll(c, 1, 0) + pltpu.roll(c, span - 1, 0)
            if r > 0:
                beside = beside + cost[r - 1]
            if r < rows - 1:
                beside = beside + cost[r + 1]
            beside = beside + jnp.where(plane > 0, pltpu.roll(c, 1, 1), 0.0)
            beside = beside + jnp.where(plane < planes - 1, pltpu.roll(c, planes - 1, 1), 0.0)
            new.append(c + rates[r] * (beside - 6.0 * c))
        cost = new

    mine = []
    for r in range(rows):
        own = cost[r][halo:halo + pix]
        for m in range(1, per_window):
            first = halo + m * pix
            own = jnp.where(lax.rem(my_block, per_window) == m, cost[r][first:first + pix], own)
        mine.append(own)
    if lanes_out > rows * pix:
        mine.append(jnp.zeros((lanes_out - rows * pix, planes), jnp.float32))
    final = jnp.concatenate(mine, axis=0).T
    peak = jnp.max(-final, axis=0, keepdims=True)
    weight = jnp.exp(-final - peak)
    denom = jnp.sum(weight, axis=0, keepdims=True)
    numer = jnp.sum(weight * depcol[...], axis=0, keepdims=True)
    depth = numer / denom
    for j in range(n):
        vs[j, 0:owned, :] = final[j * owned:(j + 1) * owned]
        vs[j, owned:owned + 1, :] = depth

    def out_copy(slot, peer):
        return pltpu.make_async_remote_copy(
            src_ref=vs.at[peer], dst_ref=out_ref.at[slot],
            send_sem=v_send.at[peer], recv_sem=v_recv.at[slot], device_id={"view": peer})

    each(1, n, lambda k: out_copy(my_block, lax.rem(me + k, n)).start())
    out_ref[my_block] = vs[me]

    def finish(k, carry):
        peer = lax.rem(me + k, n)
        aux_copy(me, peer).wait_send()
        dep_copy(me, peer).wait_send()
        feat_copy(me, peer).wait_send()
        return carry

    each(1, n, lambda k: finish(k, 0))
    each(1, groups, lambda k: half_copy(my_group, lax.rem(my_group + k, groups)).wait_send())
    each(1, rows, lambda k: cost_copy(my_row, lax.rem(my_row + k, rows)).wait_send())

    each(1, n, lambda k: out_copy(block_of(lax.rem(me - k + n, n)), lax.rem(me - k + n, n)).wait_recv())
    each(1, n, lambda k: out_copy(my_block, lax.rem(me + k, n)).wait_send())


def lay_out(pieces, cost_out, map_out):
    n = pieces.shape[0]
    owned, rows, width = cost_out.shape
    pix = width // n
    per_chunk = LANES // pix
    for c in range(width // LANES):
        at = slice(c * LANES, (c + 1) * LANES)
        if per_chunk == rows == GROUP:
            blocks = [pieces[c * rows + k, 0:owned, :] for k in range(rows)]
            lane = lax.broadcasted_iota(jnp.int32, (owned, LANES), 1) // pix
            for d in (4, 2, 1):
                upper = lax.rem(lane // d, 2) == 1
                for k in range(rows):
                    if k & d == 0:
                        a, b = blocks[k], blocks[k + d]
                        blocks[k] = jnp.where(upper, pltpu.roll(b, d * pix, 1), a)
                        blocks[k + d] = jnp.where(upper, b, pltpu.roll(a, LANES - d * pix, 1))
            for r in range(rows):
                cost_out[:, r, at] = blocks[r]
            depths = jnp.concatenate([pieces[c * rows + k, owned:, :] for k in range(rows)], axis=0)
            lane = lax.broadcasted_iota(jnp.int32, (rows, LANES), 1) // pix
            apart = lane - lax.broadcasted_iota(jnp.int32, (rows, LANES), 0)
            line = depths
            for d in range(1, rows):
                moved = pltpu.roll(pltpu.roll(depths, d * pix, 1), rows - d, 0)
                line = jnp.where(jnp.logical_or(apart == d, apart == d - rows), moved, line)
            map_out[:, at] = line
            continue
        lane = lax.broadcasted_iota(jnp.int32, (owned + 1, LANES), 1) // pix
        for r in range(rows):
            line = None
            for k in range(per_chunk):
                piece = pieces[c * per_chunk + k]
                shift = (k - r) * pix % LANES
                if shift:
                    piece = pltpu.roll(piece, shift, 1)
                line = piece if line is None else jnp.where(lane == k, piece, line)
            cost_out[:, r, at] = line[:owned]
            map_out[r:r + 1, at] = line[owned:]


def per_device(features, offsets, conf_bins, plane_depths):
    n = lax.axis_size("view")
    _, chans, rows, width = features.shape
    planes = offsets.shape[-1]
    owned = plane_depths.shape[0]
    cg = chans * rows // n
    pad = width // 8
    pix = width // n
    groups = n // rows
    step = max(GROUP, pix)
    span = step + 2 * ITERS
    reach = (rows * pix // step - 1) * step + span
    lanes_out = max(LANES, rows * pix)
    f32 = jnp.float32
    vmem = pl.BlockSpec(memory_space=pltpu.VMEM)
    dma = pltpu.SemaphoreType.DMA
    pieces = pl.pallas_call(
        functools.partial(kernel, n),
        out_shape=jax.ShapeDtypeStruct((n, owned + 1, lanes_out), f32),
        in_specs=[pl.BlockSpec(memory_space=pl.ANY), vmem, vmem, pl.BlockSpec(memory_space=pltpu.SMEM)],
        out_specs=vmem,
        scratch_shapes=[
            pltpu.VMEM((chans, rows, width), f32),
            pltpu.VMEM((n, cg, width), f32),
            pltpu.VMEM((n, cg, width), f32),
            pltpu.VMEM((n, 1, planes), jnp.int32),
            pltpu.VMEM((n, 1, planes), f32),
            pltpu.VMEM((n, 1, planes), jnp.int32),
            tuple(pltpu.SMEM((1, planes), jnp.int32) for _ in range(n)),
            pltpu.VMEM((n * pad * cg * width // LANES, LANES), f32),
            pltpu.VMEM((planes, cg * width // LANES, LANES), f32),
            pltpu.VMEM((n, width), f32),
            pltpu.VMEM((n, planes), jnp.int32),
            pltpu.VMEM((n * pad // LANES, planes, LANES), jnp.bfloat16),
            pltpu.VMEM((planes, width), f32),
            pltpu.VMEM((width + 2 * ITERS, planes), f32),
            pltpu.VMEM((groups, reach, planes), f32),
            pltpu.VMEM((reach, planes), f32),
            pltpu.VMEM((rows, span, planes), f32),
            pltpu.VMEM((width + 2 * ITERS, LANES), f32),
            pltpu.VMEM((rows, span, planes), f32),
            pltpu.VMEM((planes, lanes_out), f32),
            pltpu.VMEM((n, owned + 1, lanes_out), f32),
            dma,
        ] + [dma((n,)) for _ in range(7)] + [dma((groups,))] * 2 + [dma((rows,))] * 2 + [dma((n,))] * 2,
        compiler_params=pltpu.CompilerParams(collective_id=0, has_side_effects=True,
                                             vmem_limit_bytes=60 << 20),
    )(features, offsets, conf_bins, plane_depths)
    return pl.pallas_call(
        lay_out,
        out_shape=(
            jax.ShapeDtypeStruct((owned, rows, width), f32),
            jax.ShapeDtypeStruct((rows, width), f32),
        ),
        in_specs=[vmem],
        out_specs=(vmem, vmem),
    )(pieces)


def solution(mesh):
    in_specs = (
        P(("grp", "view"), None, None, None),
        P(("grp", "view"), None),
        P("grp", None),
        P("view"),
    )
    out_specs = (P("view", "grp", None), P("grp", None))
    return jax.shard_map(
        per_device, mesh=mesh, in_specs=in_specs, out_specs=out_specs, check_vma=False
    )
```
